256 devices in a mesh: dp: 16 (over z, core), ctx: 4 (over x), head: 4 (over y).
Axes of the slice: x: 4, y: 4, z: 8, core: 2. Of those that a mesh axis runs over, the one named last changes fastest.
Arguments:
- hidden_in: bfloat16 [16, 2048, 8192], P('dp', 'ctx', 'head'), may hold values from -40 to 40
- w_query: bfloat16 [8192, 4096], P('dp', 'head'), may hold values from -0.0625 to 0.0625
- w_key: bfloat16 [8192, 512], P('dp', 'head'), may hold values from -0.0625 to 0.0625
- w_value: bfloat16 [8192, 512], P('dp', 'head'), may hold values from -0.0625 to 0.0625
- mem_gate: float32 [32], P('head'), may hold values from -3 to 3
Outputs:
- attended: bfloat16 [16, 2048, 4096], P('dp', 'ctx', 'head')
The draws below stay inside these ranges and needn't reach their ends.
All inputs are finite; a program needn't handle non-finite values.
Results may differ from the reference program's by a relative error of at most 0.011.
Values may be sent and summed in bfloat16 or wider, within the bound.
A program may use at most 128 MiB of HBM per device.

```python
import math
import jax
import jax.numpy as jnp
from jax import lax

D = 8192
HEADS = 32
KV_HEADS = 4
HD = 128
SEG = 128
BATCH = 16
LEN = 2048


def draw_hidden_in(key, part):
    key_noise, key_topic = jax.random.split(key, 2)
    noise_part = jax.random.normal(key_noise, (BATCH, LEN, D), jnp.float32)
    topics = jax.random.normal(key_topic, (BATCH, LEN // SEG, D), jnp.float32) * 0.8
    topics = jnp.repeat(topics, SEG, axis=1)
    hidden_state = noise_part + topics
    return jnp.clip(hidden_state, -40.0, 40.0).astype(jnp.bfloat16)


def steps_of(own_key, shape, cuts, low, top_value):
    def one(axis_at, shards_of):
        heights = jax.random.uniform(jax.random.fold_in(jax.random.fold_in(own_key, 6), axis_at), (shards_of,), jnp.float32, low / len(cuts), top_value / len(cuts))
        return jnp.repeat(jnp.exp(heights), shape[axis_at] // shards_of).reshape((-1,) + (1,) * (len(shape) - axis_at - 1))

    loudness = one(*cuts[0])
    for cut in cuts[1:]:
        loudness = loudness * one(*cut)
    return loudness


def bell_draw(rng, dims, width, limit, cuts=(), dtype=jnp.bfloat16):
    values = jax.random.normal(rng, dims, jnp.float32) * width
    if len(cuts) > 0:
        values = steps_of(rng, dims, cuts, -0.22, 0.18) * values
    return jnp.clip(values, min=-limit, max=limit).astype(dtype)


def setup_inputs(seed: int = 0) -> dict:
    streams_of = jax.random.split(jax.random.key(seed), 6)
    hidden_in = draw_hidden_in(jax.random.fold_in(streams_of[5], 71), 0)
    w_query = bell_draw(streams_of[1], (D, HEADS * HD), D ** -0.5, 0.0625, ((0, 16), (1, 4)))
    w_key = bell_draw(streams_of[2], (D, KV_HEADS * HD), D ** -0.5, 0.0625, ((0, 16), (1, 4)))
    w_value = bell_draw(streams_of[3], (D, KV_HEADS * HD), D ** -0.5, 0.0625, ((0, 16), (1, 4)))
    mem_gate = jnp.clip(jax.random.uniform(streams_of[4], (HEADS,), jnp.float32, -3.0, 3.0) * steps_of(streams_of[4], (HEADS,), ((0, 4),), -0.4, 0.0), -3.0, 3.0)
    return dict(hidden_in=hidden_in, w_query=w_query, w_key=w_key, w_value=w_value, mem_gate=mem_gate)


def feature_map(vector):
    return jax.nn.elu(vector) + 1.0

def exclusive_sum(stack):
    running = jnp.cumsum(stack, axis=0)
    return jnp.concatenate([jnp.zeros_like(stack[:1]), running[:-1]], axis=0)

def one_sequence(seq_rows, w_query, w_key, w_value, mem_gate):
    highest = lax.Precision.HIGHEST
    query = jnp.dot(seq_rows, w_query, preferred_element_type=jnp.float32).astype(jnp.bfloat16)
    keys = jnp.dot(seq_rows, w_key, preferred_element_type=jnp.float32).astype(jnp.bfloat16)
    values = jnp.dot(seq_rows, w_value, preferred_element_type=jnp.float32).astype(jnp.bfloat16)
    segments = LEN // SEG
    group_size = HEADS // KV_HEADS
    query_seg = query.astype(jnp.float32).reshape(segments, SEG, KV_HEADS, group_size, HD)
    key_seg = keys.astype(jnp.float32).reshape(segments, SEG, KV_HEADS, HD)
    value_seg = values.astype(jnp.float32).reshape(segments, SEG, KV_HEADS, HD)
    scores = jnp.einsum('nqkgd,nskd->nkgqs', query_seg, key_seg) / math.sqrt(HD)
    causal = jnp.arange(SEG)[:, None] >= jnp.arange(SEG)[None, :]
    scores = jnp.where(causal, scores, -jnp.inf)
    probs = jax.nn.softmax(scores, axis=-1).astype(jnp.bfloat16).astype(jnp.float32)
    local = jnp.einsum('nkgqs,nskd->nqkgd', probs, value_seg)
    feat_key = feature_map(key_seg)
    increment = jnp.einsum('nskd,nske->nkde', feat_key, value_seg, precision=highest)
    key_mass = lax.optimization_barrier(jnp.sum(feat_key, axis=1))
    memory = exclusive_sum(increment)
    mass_prior = exclusive_sum(key_mass)
    feat_query = feature_map(query_seg)
    numerator = jnp.einsum('nqkgd,nkde->nqkge', feat_query, memory, precision=highest)
    denominator = jnp.einsum('nqkgd,nkd->nqkg', feat_query, mass_prior, precision=highest) + 1.0
    retrieved = numerator / denominator[..., None]
    gate_share = jax.nn.sigmoid(mem_gate).reshape(KV_HEADS, group_size)[None, None, :, :, None]
    mixed = gate_share * retrieved + (1.0 - gate_share) * local
    return mixed.reshape(LEN, HEADS * HD).astype(jnp.bfloat16)

def reference(hidden_in, w_query, w_key, w_value, mem_gate):
    return jnp.stack([one_sequence(hidden_in[number], w_query, w_key, w_value, mem_gate) for number in range(BATCH)], axis=0)
```

```python
import math

import jax
import jax.numpy as jnp
from jax import lax
from jax.experimental import pallas as pl
from jax.experimental.pallas import tpu as pltpu
from jax.sharding import PartitionSpec as P

HD = 128
SEG = 128
GROUP = 8
RINGZ = 8
RING = 4
ROWS = 512
COMMON = 192
QUARTER = 80
COLS = 1280
TOK = 512
FEAT = 2048
MESH = pl.DeviceIdType.MESH
LIMIT = 52 << 20
F32 = jnp.float32
BF16 = jnp.bfloat16


def kernel(
    hidden, w_query, w_key, w_value, sq, base, memory,
    w_all, h_all, acc, memaug, state, prior, before,
    load_sem, zq_s, zq_r, za_s, za_r, xq_s, xq_r, xf_s, xf_r,
    c_s, c_r, y_s, y_r, yf_s, yf_r, st_s, st_r,
):
    dp = lax.axis_index("dp")
    x = lax.axis_index("ctx")
    y = lax.axis_index("head")
    z, core = dp // 2, dp % 2

    def zdev(step):
        return {"dp": (z + RINGZ + step) % RINGZ * 2 + core}

    def xdev(step):
        return {"ctx": (x + RING + step) % RING}

    def ydev(step):
        return {"head": (y + RING + step) % RING}

    other = {"dp": z * 2 + 1 - core}
    SIGN = (1, -1)

    started = []

    def send(src, dst, ssem, rsem, dev):
        copy = pltpu.make_async_remote_copy(
            src_ref=src, dst_ref=dst, send_sem=ssem, recv_sem=rsem,
            device_id=dev, device_id_type=MESH,
        )
        copy.start()
        started.append(copy)

    def arrived(dst, ssem, rsem):
        pltpu.make_async_remote_copy(
            src_ref=dst, dst_ref=dst, send_sem=ssem, recv_sem=rsem,
            device_id=other, device_id_type=MESH,
        ).wait_recv()

    def block_of(step):
        return (z + RINGZ + step) % RINGZ * 2 + core

    def wrows(block, start, size):
        return w_all.at[pl.ds(pl.multiple_of(block * ROWS + start, 16), size), :]

    own = pl.multiple_of(dp * ROWS, ROWS)
    loads = [
        pltpu.make_async_copy(w_query, w_all.at[pl.ds(own, ROWS), 0:1024], load_sem.at[0]),
        pltpu.make_async_copy(w_key, w_all.at[pl.ds(own, ROWS), 1024:1152], load_sem.at[1]),
        pltpu.make_async_copy(w_value, w_all.at[pl.ds(own, ROWS), 1152:1280], load_sem.at[2]),
    ]
    loads.append(pltpu.make_async_copy(hidden.at[0], h_all.at[y], load_sem.at[3]))
    for load in loads:
        load.start()

    barrier = pltpu.get_barrier_semaphore()
    for peer in (zdev(1), zdev(-1), xdev(1), xdev(-1), xdev(2), ydev(1), ydev(-1), other):
        pl.semaphore_signal(barrier, inc=1, device_id=peer, device_id_type=MESH)
    pl.semaphore_wait(barrier, 8)

    def hrows(shard, start, size):
        return h_all.at[shard, pl.ds(start, size), :]

    def y_own(direction, segment):
        rows = segment * SEG, SEG
        send(
            hidden.at[0, pl.ds(*rows), :], hrows(y, *rows),
            y_s.at[direction, segment], y_r.at[direction, segment], ydev(SIGN[direction]),
        )

    def y_half(shard, direction, segment):
        return hrows(shard, segment * SEG + direction * SEG // 2, SEG // 2)

    def y_arrived(direction, segment):
        shard = (y + RING - SIGN[direction]) % RING
        arrived(
            hrows(shard, segment * SEG, SEG),
            y_s.at[direction, segment], y_r.at[direction, segment],
        )
        half = y_half(shard, direction, segment)
        send(
            half, half, yf_s.at[direction, segment], yf_r.at[direction, segment],
            ydev(SIGN[direction]),
        )

    def y_far(direction, segment):
        half = y_half((y + 2) % RING, direction, segment)
        arrived(half, yf_s.at[direction, segment], yf_r.at[direction, segment])

    for segment in range(4):
        y_own(0, segment), y_own(1, segment)

    def q_part(block, part, half):
        start, size = ((0, QUARTER), (0, 48), (48, 32))[half]
        return wrows(block, COMMON + part * QUARTER + start, size)

    def a_part(block, direction, step, piece):
        if step == 4:
            return wrows(block, direction * COMMON // 2, COMMON // 2)
        return wrows(block, (piece, 2 - piece)[direction] * COMMON // 3, COMMON // 3)

    def z_half(direction, step):
        return 0 if step < 4 else 1 + direction

    def zq_send(direction, step):
        block = block_of(-SIGN[direction] * (step - 1))
        part = q_part(block, x, z_half(direction, step))
        send(part, part, zq_s.at[direction, step - 1], zq_r.at[direction, step - 1], zdev(SIGN[direction]))

    def za_send(direction, step, piece):
        part = a_part(block_of(-SIGN[direction] * (step - 1)), direction, step, piece)
        sems = za_s.at[direction, step - 1, piece], za_r.at[direction, step - 1, piece]
        send(part, part, *sems, zdev(SIGN[direction]))

    def zq_arrived(direction, step):
        part = q_part(block_of(-SIGN[direction] * step), x, z_half(direction, step))
        arrived(part, zq_s.at[direction, step - 1], zq_r.at[direction, step - 1])
        if step < 4:
            zq_send(direction, step + 1)
        if step < 3:
            za_send(direction, 1, step)

    def za_arrived(direction, step, piece):
        part = a_part(block_of(-SIGN[direction] * step), direction, step, piece)
        sems = za_s.at[direction, step - 1, piece], za_r.at[direction, step - 1, piece]
        arrived(part, *sems)
        if step < 3:
            za_send(direction, step + 1, piece)
        elif step == 3 and piece == 1:
            za_send(direction, 4, 0)

    def x_block(i):
        return block_of((-1, 1, -2, 2, -3, 3, 4)[i])

    def xq_send(i):
        part = q_part(x_block(i), x, 0)
        for direction in (0, 1):
            send(part, part, xq_s.at[i, direction], xq_r.at[i, direction], xdev(SIGN[direction]))

    def xq_arrived(i):
        for direction in (0, 1):
            source = (x + RING - SIGN[direction]) % RING
            whole = q_part(x_block(i), source, 0)
            arrived(whole, xq_s.at[i, direction], xq_r.at[i, direction])
            part = q_part(x_block(i), source, 1 + direction)
            send(part, part, xf_s.at[i, direction], xf_r.at[i, direction], xdev(SIGN[direction]))

    def c_send(i):
        block = dp if i == 7 else x_block(i)
        part = wrows(block, 0, ROWS)
        send(part, part, c_s.at[i], c_r.at[i], other)

    def xf_arrived(i):
        for direction in (0, 1):
            part = q_part(x_block(i), (x + 2) % RING, 1 + direction)
            arrived(part, xf_s.at[i, direction], xf_r.at[i, direction])

    def c_arrived(i):
        block = dp if i == 7 else x_block(i)
        part = wrows(block + 1 - 2 * core, 0, ROWS)
        arrived(part, c_s.at[i], c_r.at[i])

    far = (y + 2) % RING

    def multiply(row, rows, block, start=0, size=COLS):
        column = pl.multiple_of(block % 4 * ROWS, ROWS)
        acc[row:row + rows, start:start + size] += jnp.dot(
            h_all[block // 4, row:row + rows, pl.ds(column, ROWS)],
            w_all[pl.ds(pl.multiple_of(block * ROWS, ROWS), ROWS), start:start + size],
            preferred_element_type=F32,
        )

    def multiply_near(step, first, last):
        def one(i, carry):
            block = (z + RINGZ + (1 - i // 2 * 2) * step) % RINGZ * 2 + i % 2

            @pl.when(block // 4 != far)
            def _():
                multiply(0, TOK, block)

            return carry

        lax.fori_loop(first, last, one, 0)

    def multiply_far(row, rows, first=0, last=4, start=0, size=COLS):
        def one(i, carry):
            multiply(row, rows, far * 4 + i, start, size)
            return carry

        lax.fori_loop(first, last, one, 0)

    def feature(v):
        return jnp.where(v > 0, v + 1.0, jnp.exp(jnp.minimum(v, 0.0)))

    iota_q = lax.broadcasted_iota(jnp.int32, (SEG, SEG), 0)
    iota_k = lax.broadcasted_iota(jnp.int32, (SEG, SEG), 1)
    scale = 1.0 / math.sqrt(HD)

    def keys_of(segment):
        rows = slice(segment * SEG, (segment + 1) * SEG)
        return acc[rows, 1024:1152].astype(BF16), acc[rows, 1152:1280].astype(BF16)

    def increment(segment):
        keys, values = keys_of(segment)
        wide = feature(keys.astype(F32))
        high = wide.astype(BF16)
        low = (wide - high.astype(F32)).astype(BF16)
        left = jnp.concatenate([values.astype(F32).T.astype(BF16), jnp.ones((HD, SEG), BF16)], axis=0)
        added = jnp.dot(left, high, preferred_element_type=F32) + jnp.dot(
            left, low, preferred_element_type=F32
        )
        memaug[segment + 1] = memaug[segment] + added

    def local(segment):
        rows = slice(segment * SEG, (segment + 1) * SEG)
        keys, values = keys_of(segment)
        values = jnp.concatenate([values, jnp.ones((SEG, HD), BF16)], axis=1)
        for h in range(GROUP):
            cols = slice(h * HD, (h + 1) * HD)
            query = acc[rows, cols].astype(BF16)
            scores = lax.dot_general(
                query, keys, (((1,), (1,)), ((), ())), preferred_element_type=F32
            ) * scale
            scores = jnp.where(iota_q >= iota_k, scores, -jnp.inf)
            top = jnp.max(scores, axis=1, keepdims=True)
            probs = jnp.exp(scores - top).astype(BF16)
            both = jnp.dot(probs, values, preferred_element_type=F32)
            base[rows, cols] = both[:, :HD] / both[:, HD:]
            sq[rows, cols] = feature(query.astype(F32)).astype(BF16)

    def state_copy(j):
        return pltpu.make_async_remote_copy(
            src_ref=state, dst_ref=prior.at[j - 1], send_sem=st_s.at[j - 1], recv_sem=st_r.at[j - 1],
            device_id=xdev(j), device_id_type=MESH,
        )

    def both_ways(f, *n):
        f(0, *n), f(1, *n)

    for load in loads:
        load.wait()
    both_ways(zq_send, 1)
    both_ways(za_send, 1, 0)
    c_send(7)
    acc[...] = jnp.zeros_like(acc)
    memaug[0] = jnp.zeros((2 * HD, HD), F32)
    before[...] = jnp.zeros_like(before)

    both_ways(zq_arrived, 1)
    xq_send(0), xq_send(1)
    xq_arrived(0)
    both_ways(zq_arrived, 2)
    xq_send(2), xq_send(3)
    xq_arrived(1)
    both_ways(zq_arrived, 3)
    both_ways(za_arrived, 1, 0)
    both_ways(za_arrived, 1, 1)
    xq_send(4), xq_send(5)
    xq_arrived(2)
    both_ways(y_arrived, 0)
    xf_arrived(0)
    both_ways(za_arrived, 1, 2)
    c_send(0)
    both_ways(y_arrived, 1)
    both_ways(zq_arrived, 4)
    xq_send(6)
    xq_arrived(3)
    xf_arrived(1)
    c_send(1)
    both_ways(za_arrived, 2, 0)
    both_ways(za_arrived, 2, 1)
    xq_arrived(4)
    both_ways(y_arrived, 2)
    both_ways(za_arrived, 2, 2)
    xq_arrived(5)
    xf_arrived(2), xf_arrived(3)
    c_send(2), c_send(3)
    both_ways(za_arrived, 3, 0)
    both_ways(za_arrived, 3, 1)
    xq_arrived(6)
    both_ways(y_arrived, 3)
    for i in (7, 0, 1):
        c_arrived(i)
    multiply_near(0, 0, 2)
    multiply_near(1, 0, 2)
    both_ways(za_arrived, 3, 2)
    xf_arrived(4), xf_arrived(5)
    c_send(4), c_send(5)
    multiply_near(1, 2, 4)
    c_arrived(2), c_arrived(3)
    multiply_near(2, 0, 2)
    both_ways(za_arrived, 4, 0)
    xf_arrived(6)
    c_send(6)
    multiply_near(2, 2, 4)
    c_arrived(4), c_arrived(5)
    multiply_near(3, 0, 4)
    c_arrived(6)
    multiply_near(4, 0, 2)
    both_ways(y_far, 0), both_ways(y_far, 1)
    multiply_far(0, 256)
    for segment in (0, 1):
        increment(segment)
        local(segment)
    both_ways(y_far, 2)
    multiply_far(256, 128)
    increment(2)
    local(2)
    both_ways(y_far, 3)
    multiply_far(384, 128, 0, 4, 1024, 256)
    increment(3)
    state[...] = memaug[4, :HD + 16].astype(BF16)
    multiply_far(384, 128, 0, 1, 0, 1024)
    for j in (1, 2, 3):
        @pl.when(x + j < RING)
        def _():
            state_copy(j).start()
    multiply_far(384, 128, 1, 4, 0, 1024)
    local(3)
    for j in (1, 2, 3):
        @pl.when(x >= j)
        def _():
            state_copy(j).wait_recv()
            before[:HD] += prior[j - 1, :HD].astype(F32)
            before[HD:] += prior[j - 1, HD:HD + 1].astype(F32)
    for segment in range(4):
        memory[segment] = (memaug[segment] + before[...]).astype(BF16)
    for copy in started:
        copy.wait_send()
    for j in (1, 2, 3):
        @pl.when(x + j < RING)
        def _():
            state_copy(j).wait_send()


def share(gate, h):
    return jax.nn.sigmoid(jnp.full((1, HD), gate[h], F32))


def finish(sq, base, memory, gate, out):
    for h in range(GROUP):
        cols = slice(h * HD, (h + 1) * HD)
        both = lax.dot_general(
            sq[:, cols], memory[0], (((1,), (1,)), ((), ())), preferred_element_type=F32
        )
        part = share(gate, h)
        retrieved = both[:, :HD] / (both[:, HD:] + 1.0)
        out[0, :, cols] = (part * retrieved + (1.0 - part) * base[:, cols]).astype(BF16)


def body(hidden_in, w_query, w_key, w_value, mem_gate):
    dma = pltpu.SemaphoreType.DMA
    anywhere = pl.BlockSpec(memory_space=pl.ANY)
    width = GROUP * HD
    results = pl.pallas_call(
        kernel,
        out_shape=(
            pltpu.VMEM((TOK, width), BF16),
            pltpu.VMEM((TOK, width), F32),
            pltpu.VMEM((4, 2 * HD, HD), BF16),
        ),
        in_specs=[anywhere] * 4,
        out_specs=[pl.BlockSpec(memory_space=pltpu.VMEM)] * 3,
        scratch_shapes=[
            pltpu.VMEM((16 * ROWS, COLS), BF16),
            pltpu.VMEM((RING, TOK, FEAT), BF16),
            pltpu.VMEM((TOK, COLS), F32),
            pltpu.VMEM((5, 2 * HD, HD), F32),
            pltpu.VMEM((HD + 16, HD), BF16),
            pltpu.VMEM((3, HD + 16, HD), BF16),
            pltpu.VMEM((2 * HD, HD), F32),
            dma((4,)), dma((2, 4)), dma((2, 4)), dma((2, 4, 3)), dma((2, 4, 3)),
            dma((7, 2)), dma((7, 2)), dma((7, 2)), dma((7, 2)),
            dma((8,)), dma((8,)), dma((2, 4)), dma((2, 4)), dma((2, 4)), dma((2, 4)),
            dma((3,)), dma((3,)),
        ],
        compiler_params=pltpu.CompilerParams(
            collective_id=0, has_side_effects=True, vmem_limit_bytes=LIMIT
        ),
    )(*[pltpu.with_memory_space_constraint(a, pltpu.HBM) for a in (hidden_in, w_query, w_key, w_value)])
    return pl.pallas_call(
        finish,
        grid=(4,),
        out_shape=jax.ShapeDtypeStruct((1, TOK, width), BF16),
        in_specs=[
            pl.BlockSpec((SEG, width), lambda i: (i, 0)),
            pl.BlockSpec((SEG, width), lambda i: (i, 0)),
            pl.BlockSpec((1, 2 * HD, HD), lambda i: (i, 0, 0)),
            pl.BlockSpec(memory_space=pltpu.SMEM),
        ],
        out_specs=pl.BlockSpec((1, SEG, width), lambda i: (0, i, 0)),
        compiler_params=pltpu.CompilerParams(vmem_limit_bytes=8 << 20),
    )(*results, mem_gate)


def solution(mesh):
    return jax.shard_map(
        body,
        mesh=mesh,
        in_specs=(
            P("dp", "ctx", "head"),
            P("dp", "head"),
            P("dp", "head"),
            P("dp", "head"),
            P("head"),
        ),
        out_specs=P("dp", "ctx", "head"),
        check_vma=False,
    )
```

```python
import math

import jax
import jax.numpy as jnp
from jax import lax
from jax.experimental import pallas as pl
from jax.experimental.pallas import tpu as pltpu
from jax.sharding import PartitionSpec as P

HD = 128
SEG = 128
GROUP = 8
RINGZ = 8
RING = 4
ROWS = 512
COMMON = 192
QUARTER = 80
COLS = 1280
TOK = 512
FEAT = 2048
MESH = pl.DeviceIdType.MESH
LIMIT = 52 << 20
F32 = jnp.float32
BF16 = jnp.bfloat16


def kernel(
    hidden, w_query, w_key, w_value, sq, base, memory,
    w_all, h_all, acc, memaug, state, prior, before,
    load_sem, zq_s, zq_r, za_s, za_r, xq_s, xq_r, xf_s, xf_r,
    c_s, c_r, y_s, y_r, yf_s, yf_r, st_s, st_r,
):
    dp = lax.axis_index("dp")
    x = lax.axis_index("ctx")
    y = lax.axis_index("head")
    z, core = dp // 2, dp % 2

    def zdev(step):
        return {"dp": (z + RINGZ + step) % RINGZ * 2 + core}

    def xdev(step):
        return {"ctx": (x + RING + step) % RING}

    def ydev(step):
        return {"head": (y + RING + step) % RING}

    other = {"dp": z * 2 + 1 - core}
    SIGN = (1, -1)

    started = []

    def send(src, dst, ssem, rsem, dev):
        copy = pltpu.make_async_remote_copy(
            src_ref=src, dst_ref=dst, send_sem=ssem, recv_sem=rsem,
            device_id=dev, device_id_type=MESH,
        )
        copy.start()
        started.append(copy)

    def arrived(dst, ssem, rsem):
        pltpu.make_async_remote_copy(
            src_ref=dst, dst_ref=dst, send_sem=ssem, recv_sem=rsem,
            device_id=other, device_id_type=MESH,
        ).wait_recv()

    def block_of(step):
        return (z + RINGZ + step) % RINGZ * 2 + core

    def wrows(block, start, size):
        return w_all.at[pl.ds(pl.multiple_of(block * ROWS + start, 16), size), :]

    own = pl.multiple_of(dp * ROWS, ROWS)
    loads = [
        pltpu.make_async_copy(w_query, w_all.at[pl.ds(own, ROWS), 0:1024], load_sem.at[0]),
        pltpu.make_async_copy(w_key, w_all.at[pl.ds(own, ROWS), 1024:1152], load_sem.at[1]),
        pltpu.make_async_copy(w_value, w_all.at[pl.ds(own, ROWS), 1152:1280], load_sem.at[2]),
    ]
    loads.append(pltpu.make_async_copy(hidden.at[0], h_all.at[y], load_sem.at[3]))
    for load in loads:
        load.start()

    barrier = pltpu.get_barrier_semaphore()
    for peer in (zdev(1), zdev(-1), xdev(1), xdev(-1), xdev(2), ydev(1), ydev(-1), other):
        pl.semaphore_signal(barrier, inc=1, device_id=peer, device_id_type=MESH)
    pl.semaphore_wait(barrier, 8)

    def hrows(shard, start, size):
        return h_all.at[shard, pl.ds(start, size), :]

    def y_own(direction, segment):
        rows = segment * SEG, SEG
        send(
            hidden.at[0, pl.ds(*rows), :], hrows(y, *rows),
            y_s.at[direction, segment], y_r.at[direction, segment], ydev(SIGN[direction]),
        )

    def y_half(shard, direction, segment):
        return hrows(shard, segment * SEG + direction * SEG // 2, SEG // 2)

    def y_arrived(direction, segment):
        shard = (y + RING - SIGN[direction]) % RING
        arrived(
            hrows(shard, segment * SEG, SEG),
            y_s.at[direction, segment], y_r.at[direction, segment],
        )
        half = y_half(shard, direction, segment)
        send(
            half, half, yf_s.at[direction, segment], yf_r.at[direction, segment],
            ydev(SIGN[direction]),
        )

    def y_far(direction, segment):
        half = y_half((y + 2) % RING, direction, segment)
        arrived(half, yf_s.at[direction, segment], yf_r.at[direction, segment])

    for segment in range(4):
        y_own(0, segment), y_own(1, segment)

    def q_part(block, part, half):
        start, size = ((0, QUARTER), (0, 48), (48, 32), (0, 32), (32, 48))[half]
        return wrows(block, COMMON + part * QUARTER + start, size)

    def a_part(block, direction, step, piece):
        if step == 4:
            return wrows(block, direction * COMMON // 2, COMMON // 2)
        return wrows(block, (piece, 2 - piece)[direction] * COMMON // 3, COMMON // 3)

    def z_half(direction, step):
        return 0 if step < 4 else 1 + direction

    def zq_send(direction, step):
        block = block_of(-SIGN[direction] * (step - 1))
        part = q_part(block, x, z_half(direction, step))
        send(part, part, zq_s.at[direction, step - 1], zq_r.at[direction, step - 1], zdev(SIGN[direction]))

    def za_send(direction, step, piece):
        part = a_part(block_of(-SIGN[direction] * (step - 1)), direction, step, piece)
        sems = za_s.at[direction, step - 1, piece], za_r.at[direction, step - 1, piece]
        send(part, part, *sems, zdev(SIGN[direction]))

    def zq_arrived(direction, step):
        part = q_part(block_of(-SIGN[direction] * step), x, z_half(direction, step))
        arrived(part, zq_s.at[direction, step - 1], zq_r.at[direction, step - 1])
        if step < 4:
            zq_send(direction, step + 1)
        if step == 1:
            za_send(direction, 1, 2)

    def za_arrived(direction, step, piece):
        part = a_part(block_of(-SIGN[direction] * step), direction, step, piece)
        sems = za_s.at[direction, step - 1, piece], za_r.at[direction, step - 1, piece]
        arrived(part, *sems)
        if step < 3:
            za_send(direction, step + 1, piece)
        elif step == 3 and piece == 1:
            za_send(direction, 4, 0)

    def x_block(i):
        return block_of((-1, 1, -2, 2, -3, 3, 4)[i])

    def xq_send(i):
        part = q_part(x_block(i), x, 0)
        for direction in (0, 1):
            send(part, part, xq_s.at[i, direction], xq_r.at[i, direction], xdev(SIGN[direction]))

    def xq_arrived(i):
        for direction in (0, 1):
            source = (x + RING - SIGN[direction]) % RING
            whole = q_part(x_block(i), source, 0)
            arrived(whole, xq_s.at[i, direction], xq_r.at[i, direction])
            part = q_part(x_block(i), source, 1 + direction + i % 2 * 2)
            send(part, part, xf_s.at[i, direction], xf_r.at[i, direction], xdev(SIGN[direction]))

    def c_part(block, part):
        start, size = ((0, COMMON), (COMMON, ROWS - COMMON))[part]
        return wrows(block, start, size)

    def c_send(i, part):
        rows = c_part(dp if i == 7 else x_block(i), part)
        send(rows, rows, c_s.at[i, part], c_r.at[i, part], other)

    def xf_arrived(i):
        for direction in (0, 1):
            part = q_part(x_block(i), (x + 2) % RING, 1 + direction + i % 2 * 2)
            arrived(part, xf_s.at[i, direction], xf_r.at[i, direction])

    def c_arrived(i):
        block = dp if i == 7 else x_block(i)
        for part in (0, 1):
            arrived(c_part(block + 1 - 2 * core, part), c_s.at[i, part], c_r.at[i, part])

    far = (y + 2) % RING

    def multiply(row, rows, block, start=0, size=COLS):
        column = pl.multiple_of(block % 4 * ROWS, ROWS)
        acc[row:row + rows, start:start + size] += jnp.dot(
            h_all[block // 4, row:row + rows, pl.ds(column, ROWS)],
            w_all[pl.ds(pl.multiple_of(block * ROWS, ROWS), ROWS), start:start + size],
            preferred_element_type=F32,
        )

    def multiply_near(step, first, last):
        def one(i, carry):
            block = (z + RINGZ + (1 - i // 2 * 2) * step) % RINGZ * 2 + i % 2

            @pl.when(block // 4 != far)
            def _():
                multiply(0, TOK, block)

            return carry

        lax.fori_loop(first, last, one, 0)

    opposite = (z + 4) % RINGZ

    def multiply_far(row, rows, first=0, last=4, start=0, size=COLS, late=None):
        def one(i, carry):
            block = far * 4 + i
            if late is None:
                multiply(row, rows, block, start, size)
            else:
                @pl.when((block // 2 == opposite) == late)
                def _():
                    multiply(row, rows, block, start, size)
            return carry

        lax.fori_loop(first, last, one, 0)

    def feature(v):
        return jnp.where(v > 0, v + 1.0, jnp.exp(jnp.minimum(v, 0.0)))

    iota_q = lax.broadcasted_iota(jnp.int32, (SEG, SEG), 0)
    iota_k = lax.broadcasted_iota(jnp.int32, (SEG, SEG), 1)
    scale = 1.0 / math.sqrt(HD)

    def keys_of(segment):
        rows = slice(segment * SEG, (segment + 1) * SEG)
        return acc[rows, 1024:1152].astype(BF16), acc[rows, 1152:1280].astype(BF16)

    def increment(segment):
        keys, values = keys_of(segment)
        wide = feature(keys.astype(F32))
        high = wide.astype(BF16)
        low = (wide - high.astype(F32)).astype(BF16)
        left = jnp.concatenate([values.astype(F32).T.astype(BF16), jnp.ones((HD, SEG), BF16)], axis=0)
        added = jnp.dot(left, high, preferred_element_type=F32) + jnp.dot(
            left, low, preferred_element_type=F32
        )
        memaug[segment + 1] = memaug[segment] + added

    def local(segment):
        rows = slice(segment * SEG, (segment + 1) * SEG)
        keys, values = keys_of(segment)
        values = jnp.concatenate([values, jnp.ones((SEG, HD), BF16)], axis=1)
        for h in range(GROUP):
            cols = slice(h * HD, (h + 1) * HD)
            query = acc[rows, cols].astype(BF16)
            scores = lax.dot_general(
                query, keys, (((1,), (1,)), ((), ())), preferred_element_type=F32
            ) * scale
            scores = jnp.where(iota_q >= iota_k, scores, -jnp.inf)
            top = jnp.max(scores, axis=1, keepdims=True)
            probs = jnp.exp(scores - top).astype(BF16)
            both = jnp.dot(probs, values, preferred_element_type=F32)
            base[rows, cols] = both[:, :HD] / both[:, HD:]
            sq[rows, cols] = feature(query.astype(F32)).astype(BF16)

    def state_copy(j):
        return pltpu.make_async_remote_copy(
            src_ref=state, dst_ref=prior.at[j - 1], send_sem=st_s.at[j - 1], recv_sem=st_r.at[j - 1],
            device_id=xdev(j), device_id_type=MESH,
        )

    def both_ways(f, *n):
        f(0, *n), f(1, *n)

    for load in loads:
        load.wait()
    both_ways(zq_send, 1)
    both_ways(za_send, 1, 0)
    both_ways(za_send, 1, 1)
    c_send(7, 0), c_send(7, 1)
    acc[...] = jnp.zeros_like(acc)
    memaug[0] = jnp.zeros((2 * HD, HD), F32)
    before[...] = jnp.zeros_like(before)

    both_ways(zq_arrived, 1)
    xq_send(0), xq_send(1)
    both_ways(za_arrived, 1, 0)
    xq_arrived(0)
    both_ways(y_arrived, 0)
    xq_arrived(1)
    both_ways(zq_arrived, 2)
    xq_send(2), xq_send(3)
    both_ways(za_arrived, 1, 1)
    xf_arrived(0)
    c_send(0, 1)
    both_ways(za_arrived, 1, 2)
    c_send(0, 0), c_send(1, 0)
    xf_arrived(1)
    c_send(1, 1)
    both_ways(y_arrived, 1)
    xq_arrived(2)
    both_ways(zq_arrived, 3)
    xq_arrived(3)
    xq_send(4), xq_send(5)
    both_ways(za_arrived, 2, 0)
    both_ways(za_arrived, 2, 1)
    xf_arrived(2), xf_arrived(3)
    c_send(2, 1), c_send(3, 1)
    both_ways(za_arrived, 2, 2)
    c_send(2, 0), c_send(3, 0)
    both_ways(y_arrived, 2)
    xq_arrived(4)
    both_ways(zq_arrived, 4)
    xq_send(6)
    xq_arrived(5)
    both_ways(za_arrived, 3, 0)
    both_ways(za_arrived, 3, 1)
    xf_arrived(4), xf_arrived(5)
    c_send(4, 1), c_send(5, 1)
    both_ways(y_arrived, 3)
    xq_arrived(6)
    for i in (7, 0, 1):
        c_arrived(i)
    multiply_near(0, 0, 2)
    both_ways(za_arrived, 3, 2)
    c_send(4, 0), c_send(5, 0)
    multiply_near(1, 0, 4)
    xf_arrived(6)
    c_send(6, 1)
    c_arrived(2), c_arrived(3)
    multiply_near(2, 0, 2)
    both_ways(za_arrived, 4, 0)
    c_send(6, 0)
    multiply_near(2, 2, 4)
    c_arrived(4), c_arrived(5)
    multiply_near(3, 0, 4)
    both_ways(y_far, 0), both_ways(y_far, 1)
    multiply_far(0, 256, late=False)
    c_arrived(6)
    multiply_far(0, 256, late=True)
    multiply_near(4, 0, 2)
    for segment in (0, 1):
        increment(segment)
        local(segment)
    both_ways(y_far, 2)
    multiply_far(256, 128)
    increment(2)
    local(2)
    both_ways(y_far, 3)
    multiply_far(384, 128, 0, 4, 1024, 256)
    increment(3)
    state[...] = memaug[4, :HD + 16].astype(BF16)
    multiply_far(384, 128, 0, 1, 0, 1024)
    for j in (1, 2, 3):
        @pl.when(x + j < RING)
        def _():
            state_copy(j).start()
    multiply_far(384, 128, 1, 4, 0, 1024)
    local(3)
    for j in (1, 2, 3):
        @pl.when(x >= j)
        def _():
            state_copy(j).wait_recv()
            before[:HD] += prior[j - 1, :HD].astype(F32)
            before[HD:] += prior[j - 1, HD:HD + 1].astype(F32)
    for segment in range(4):
        memory[segment] = (memaug[segment] + before[...]).astype(BF16)
    for copy in started:
        copy.wait_send()
    for j in (1, 2, 3):
        @pl.when(x + j < RING)
        def _():
            state_copy(j).wait_send()


def share(gate, h):
    return jax.nn.sigmoid(jnp.full((1, HD), gate[h], F32))


def finish(sq, base, memory, gate, out, mixed, sem):
    copies = []
    for segment in range(TOK // SEG):
        rows = slice(segment * SEG, (segment + 1) * SEG)
        for h in range(GROUP):
            cols = slice(h * HD, (h + 1) * HD)
            both = lax.dot_general(
                sq[rows, cols], memory[segment], (((1,), (1,)), ((), ())), preferred_element_type=F32
            )
            part = share(gate, h)
            retrieved = both[:, :HD] / (both[:, HD:] + 1.0)
            mixed[rows, cols] = (part * retrieved + (1.0 - part) * base[rows, cols]).astype(BF16)
        copies.append(pltpu.make_async_copy(mixed.at[rows, :], out.at[0, rows, :], sem.at[segment]))
        copies[-1].start()
    for copy in copies:
        copy.wait()


def body(hidden_in, w_query, w_key, w_value, mem_gate):
    dma = pltpu.SemaphoreType.DMA
    anywhere = pl.BlockSpec(memory_space=pl.ANY)
    width = GROUP * HD
    results = pl.pallas_call(
        kernel,
        out_shape=(
            pltpu.VMEM((TOK, width), BF16),
            pltpu.VMEM((TOK, width), F32),
            pltpu.VMEM((4, 2 * HD, HD), BF16),
        ),
        in_specs=[anywhere] * 4,
        out_specs=[pl.BlockSpec(memory_space=pltpu.VMEM)] * 3,
        scratch_shapes=[
            pltpu.VMEM((16 * ROWS, COLS), BF16),
            pltpu.VMEM((RING, TOK, FEAT), BF16),
            pltpu.VMEM((TOK, COLS), F32),
            pltpu.VMEM((5, 2 * HD, HD), F32),
            pltpu.VMEM((HD + 16, HD), BF16),
            pltpu.VMEM((3, HD + 16, HD), BF16),
            pltpu.VMEM((2 * HD, HD), F32),
            dma((4,)), dma((2, 4)), dma((2, 4)), dma((2, 4, 3)), dma((2, 4, 3)),
            dma((7, 2)), dma((7, 2)), dma((7, 2)), dma((7, 2)),
            dma((8, 2)), dma((8, 2)), dma((2, 4)), dma((2, 4)), dma((2, 4)), dma((2, 4)),
            dma((3,)), dma((3,)),
        ],
        compiler_params=pltpu.CompilerParams(
            collective_id=0, has_side_effects=True, vmem_limit_bytes=LIMIT
        ),
    )(*[pltpu.with_memory_space_constraint(a, pltpu.HBM) for a in (hidden_in, w_query, w_key, w_value)])
    vmem = pl.BlockSpec(memory_space=pltpu.VMEM)
    return pl.pallas_call(
        finish,
        out_shape=jax.ShapeDtypeStruct((1, TOK, width), BF16),
        in_specs=[vmem, vmem, vmem, pl.BlockSpec(memory_space=pltpu.SMEM)],
        out_specs=anywhere,
        scratch_shapes=[pltpu.VMEM((TOK, width), BF16), dma((4,))],
        compiler_params=pltpu.CompilerParams(vmem_limit_bytes=8 << 20),
    )(*results, mem_gate)


def solution(mesh):
    return jax.shard_map(
        body,
        mesh=mesh,
        in_specs=(
            P("dp", "ctx", "head"),
            P("dp", "head"),
            P("dp", "head"),
            P("dp", "head"),
            P("head"),
        ),
        out_specs=P("dp", "ctx", "head"),
        check_vma=False,
    )
```

```python
import math

import jax
import jax.numpy as jnp
from jax import lax
from jax.experimental import pallas as pl
from jax.experimental.pallas import tpu as pltpu
from jax.sharding import PartitionSpec as P

HD = 128
SEG = 128
GROUP = 8
RINGZ = 8
RING = 4
ROWS = 512
COMMON = 192
QUARTER = 80
COLS = 1280
TOK = 512
FEAT = 2048
MESH = pl.DeviceIdType.MESH
LIMIT = 52 << 20
F32 = jnp.float32
BF16 = jnp.bfloat16


def kernel(
    hidden, w_query, w_key, w_value, sq, base, memory,
    w_all, h_all, acc, memaug, state, prior, before,
    load_sem, zq_s, zq_r, za_s, za_r, xq_s, xq_r, xf_s, xf_r,
    c_s, c_r, y_s, y_r, yf_s, yf_r, st_s, st_r,
):
    dp = lax.axis_index("dp")
    x = lax.axis_index("ctx")
    y = lax.axis_index("head")
    z, core = dp // 2, dp % 2

    def zdev(step):
        return {"dp": (z + RINGZ + step) % RINGZ * 2 + core}

    def xdev(step):
        return {"ctx": (x + RING + step) % RING}

    def ydev(step):
        return {"head": (y + RING + step) % RING}

    other = {"dp": z * 2 + 1 - core}
    SIGN = (1, -1)

    started, forwarded = [], []

    def send(src, dst, ssem, rsem, dev, held=None):
        copy = pltpu.make_async_remote_copy(
            src_ref=src, dst_ref=dst, send_sem=ssem, recv_sem=rsem,
            device_id=dev, device_id_type=MESH,
        )
        copy.start()
        (started if held is None else held).append(copy)

    def arrived(dst, ssem, rsem):
        pltpu.make_async_remote_copy(
            src_ref=dst, dst_ref=dst, send_sem=ssem, recv_sem=rsem,
            device_id=other, device_id_type=MESH,
        ).wait_recv()

    def block_of(step):
        return (z + RINGZ + step) % RINGZ * 2 + core

    def wrows(block, start, size):
        return w_all.at[pl.ds(pl.multiple_of(block * ROWS + start, 16), size), :]

    own = pl.multiple_of(dp * ROWS, ROWS)
    loads = [
        pltpu.make_async_copy(w_query, w_all.at[pl.ds(own, ROWS), 0:1024], load_sem.at[0]),
        pltpu.make_async_copy(w_key, w_all.at[pl.ds(own, ROWS), 1024:1152], load_sem.at[1]),
        pltpu.make_async_copy(w_value, w_all.at[pl.ds(own, ROWS), 1152:1280], load_sem.at[2]),
    ]
    loads.append(pltpu.make_async_copy(hidden.at[0], h_all.at[y], load_sem.at[3]))
    for load in loads:
        load.start()

    barrier = pltpu.get_barrier_semaphore()
    for peer in (zdev(1), zdev(-1), xdev(1), xdev(-1), xdev(2), ydev(1), ydev(-1), other):
        pl.semaphore_signal(barrier, inc=1, device_id=peer, device_id_type=MESH)
    pl.semaphore_wait(barrier, 8)

    def hrows(shard, start, size):
        return h_all.at[shard, pl.ds(start, size), :]

    def y_own(direction, segment):
        rows = segment * SEG, SEG
        send(
            hidden.at[0, pl.ds(*rows), :], hrows(y, *rows),
            y_s.at[direction, segment], y_r.at[direction, segment], ydev(SIGN[direction]),
        )

    def y_half(shard, direction, piece):
        if piece >= 3:
            columns = pl.ds((2 * direction + piece - 3) * ROWS, ROWS)
            return h_all.at[shard, pl.ds(3 * SEG, SEG), columns]
        return hrows(shard, piece * SEG + direction * SEG // 2, SEG // 2)

    def y_arrived(direction, segment):
        shard = (y + RING - SIGN[direction]) % RING
        arrived(
            hrows(shard, segment * SEG, SEG),
            y_s.at[direction, segment], y_r.at[direction, segment],
        )
        for piece in (3, 4) if segment == 3 else (segment,):
            half = y_half(shard, direction, piece)
            send(
                half, half, yf_s.at[direction, piece], yf_r.at[direction, piece],
                ydev(SIGN[direction]), forwarded,
            )

    def y_far(direction, piece):
        half = y_half((y + 2) % RING, direction, piece)
        arrived(half, yf_s.at[direction, piece], yf_r.at[direction, piece])

    for segment in range(4):
        y_own(0, segment), y_own(1, segment)

    def q_part(block, part, half):
        start, size = ((0, QUARTER), (0, 48), (48, 32), (0, 32), (32, 48))[half]
        return wrows(block, COMMON + part * QUARTER + start, size)

    def a_part(block, direction, step, piece):
        if step == 4:
            return wrows(block, direction * COMMON // 2, COMMON // 2)
        return wrows(block, (piece, 2 - piece)[direction] * COMMON // 3, COMMON // 3)

    def z_half(direction, step):
        return 0 if step < 4 else 1 + direction

    def zq_send(direction, step):
        block = block_of(-SIGN[direction] * (step - 1))
        part = q_part(block, x, z_half(direction, step))
        send(part, part, zq_s.at[direction, step - 1], zq_r.at[direction, step - 1], zdev(SIGN[direction]))

    def za_send(direction, step, piece):
        part = a_part(block_of(-SIGN[direction] * (step - 1)), direction, step, piece)
        sems = za_s.at[direction, step - 1, piece], za_r.at[direction, step - 1, piece]
        send(part, part, *sems, zdev(SIGN[direction]))

    def zq_arrived(direction, step):
        part = q_part(block_of(-SIGN[direction] * step), x, z_half(direction, step))
        arrived(part, zq_s.at[direction, step - 1], zq_r.at[direction, step - 1])
        if step < 4:
            zq_send(direction, step + 1)
        if step == 1:
            za_send(direction, 1, 2)

    def za_arrived(direction, step, piece):
        part = a_part(block_of(-SIGN[direction] * step), direction, step, piece)
        sems = za_s.at[direction, step - 1, piece], za_r.at[direction, step - 1, piece]
        arrived(part, *sems)
        if step < 3:
            za_send(direction, step + 1, piece)
        elif step == 3 and piece == 1:
            za_send(direction, 4, 0)

    def x_block(i):
        return block_of((-1, 1, -2, 2, -3, 3, 4)[i])

    def xq_send(i):
        part = q_part(x_block(i), x, 0)
        for direction in (0, 1):
            send(part, part, xq_s.at[i, direction], xq_r.at[i, direction], xdev(SIGN[direction]))

    def xq_arrived(i):
        for direction in (0, 1):
            source = (x + RING - SIGN[direction]) % RING
            whole = q_part(x_block(i), source, 0)
            arrived(whole, xq_s.at[i, direction], xq_r.at[i, direction])
            part = q_part(x_block(i), source, 1 + direction + i % 2 * 2)
            send(part, part, xf_s.at[i, direction], xf_r.at[i, direction], xdev(SIGN[direction]))

    def c_part(block, part):
        start, size = ((0, COMMON), (COMMON, ROWS - COMMON))[part]
        return wrows(block, start, size)

    def c_send(i, part):
        rows = c_part(dp if i == 7 else x_block(i), part)
        send(rows, rows, c_s.at[i, part], c_r.at[i, part], other)

    def xf_arrived(i):
        for direction in (0, 1):
            part = q_part(x_block(i), (x + 2) % RING, 1 + direction + i % 2 * 2)
            arrived(part, xf_s.at[i, direction], xf_r.at[i, direction])

    def c_arrived(i):
        block = dp if i == 7 else x_block(i)
        for part in (0, 1):
            arrived(c_part(block + 1 - 2 * core, part), c_s.at[i, part], c_r.at[i, part])

    far = (y + 2) % RING

    def multiply(row, rows, block, start=0, size=COLS):
        column = pl.multiple_of(block % 4 * ROWS, ROWS)
        acc[row:row + rows, start:start + size] += jnp.dot(
            h_all[block // 4, row:row + rows, pl.ds(column, ROWS)],
            w_all[pl.ds(pl.multiple_of(block * ROWS, ROWS), ROWS), start:start + size],
            preferred_element_type=F32,
        )

    def multiply_near(step, first, last):
        def one(i, carry):
            block = (z + RINGZ + (1 - i // 2 * 2) * step) % RINGZ * 2 + i % 2

            @pl.when(block // 4 != far)
            def _():
                multiply(0, TOK, block)

            return carry

        lax.fori_loop(first, last, one, 0)

    opposite = (z + 4) % RINGZ

    def multiply_far(row, rows, first=0, last=4, start=0, size=COLS, late=None):
        def one(i, carry):
            block = far * 4 + i
            if late is None:
                multiply(row, rows, block, start, size)
            else:
                @pl.when((block // 2 == opposite) == late)
                def _():
                    multiply(row, rows, block, start, size)
            return carry

        lax.fori_loop(first, last, one, 0)

    def feature(v):
        return jnp.where(v > 0, v + 1.0, jnp.exp(jnp.minimum(v, 0.0)))

    iota_q = lax.broadcasted_iota(jnp.int32, (SEG, SEG), 0)
    iota_k = lax.broadcasted_iota(jnp.int32, (SEG, SEG), 1)
    scale = 1.0 / math.sqrt(HD)

    def multiply_last(first, last, odd, start, size):
        def one(i, carry):
            multiply(384, 128, far * 4 + 2 * i + odd, start, size)
            return carry

        lax.fori_loop(first, last, one, 0)

    def keys_of(segment):
        rows = slice(segment * SEG, (segment + 1) * SEG)
        return acc[rows, 1024:1152].astype(BF16), acc[rows, 1152:1280].astype(BF16)

    def increment(segment):
        keys, values = keys_of(segment)
        wide = feature(keys.astype(F32))
        high = wide.astype(BF16)
        low = (wide - high.astype(F32)).astype(BF16)
        left = jnp.concatenate([values.astype(F32).T.astype(BF16), jnp.ones((HD, SEG), BF16)], axis=0)
        added = jnp.dot(left, high, preferred_element_type=F32) + jnp.dot(
            left, low, preferred_element_type=F32
        )
        memaug[segment + 1] = memaug[segment] + added

    def local(segment):
        rows = slice(segment * SEG, (segment + 1) * SEG)
        keys, values = keys_of(segment)
        values = jnp.concatenate([values, jnp.ones((SEG, HD), BF16)], axis=1)
        for h in range(GROUP):
            cols = slice(h * HD, (h + 1) * HD)
            query = acc[rows, cols].astype(BF16)
            scores = lax.dot_general(
                query, keys, (((1,), (1,)), ((), ())), preferred_element_type=F32
            ) * scale
            scores = jnp.where(iota_q >= iota_k, scores, -jnp.inf)
            top = jnp.max(scores, axis=1, keepdims=True)
            probs = jnp.exp(scores - top).astype(BF16)
            both = jnp.dot(probs, values, preferred_element_type=F32)
            base[rows, cols] = both[:, :HD] / both[:, HD:]
            sq[rows, cols] = feature(query.astype(F32)).astype(BF16)

    def state_copy(j):
        return pltpu.make_async_remote_copy(
            src_ref=state, dst_ref=prior.at[j - 1], send_sem=st_s.at[j - 1], recv_sem=st_r.at[j - 1],
            device_id=xdev(j), device_id_type=MESH,
        )

    def both_ways(f, *n):
        f(0, *n), f(1, *n)

    for load in loads:
        load.wait()
    both_ways(zq_send, 1)
    both_ways(za_send, 1, 0)
    both_ways(za_send, 1, 1)
    c_send(7, 0), c_send(7, 1)
    acc[...] = jnp.zeros_like(acc)
    memaug[0] = jnp.zeros((2 * HD, HD), F32)
    before[...] = jnp.zeros_like(before)

    both_ways(zq_arrived, 1)
    xq_send(0), xq_send(1)
    both_ways(za_arrived, 1, 0)
    xq_arrived(0)
    both_ways(y_arrived, 0)
    xq_arrived(1)
    both_ways(zq_arrived, 2)
    xq_send(2), xq_send(3)
    both_ways(za_arrived, 1, 1)
    xf_arrived(0)
    c_send(0, 1)
    both_ways(za_arrived, 1, 2)
    c_send(0, 0), c_send(1, 0)
    xf_arrived(1)
    c_send(1, 1)
    both_ways(y_arrived, 1)
    xq_arrived(2)
    both_ways(zq_arrived, 3)
    xq_arrived(3)
    xq_send(4), xq_send(5)
    both_ways(za_arrived, 2, 0)
    both_ways(za_arrived, 2, 1)
    xf_arrived(2), xf_arrived(3)
    c_send(2, 1), c_send(3, 1)
    both_ways(za_arrived, 2, 2)
    c_send(2, 0), c_send(3, 0)
    both_ways(y_arrived, 2)
    xq_arrived(4)
    both_ways(zq_arrived, 4)
    xq_send(6)
    xq_arrived(5)
    both_ways(za_arrived, 3, 0)
    both_ways(za_arrived, 3, 1)
    xf_arrived(4), xf_arrived(5)
    c_send(4, 1), c_send(5, 1)
    both_ways(y_arrived, 3)
    xq_arrived(6)
    for i in (7, 0, 1):
        c_arrived(i)
    multiply_near(0, 0, 2)
    both_ways(za_arrived, 3, 2)
    c_send(4, 0), c_send(5, 0)
    multiply_near(1, 0, 4)
    xf_arrived(6)
    c_send(6, 1)
    c_arrived(2), c_arrived(3)
    multiply_near(2, 0, 2)
    both_ways(za_arrived, 4, 0)
    c_send(6, 0)
    multiply_near(2, 2, 4)
    c_arrived(4), c_arrived(5)
    multiply_near(3, 0, 4)
    both_ways(y_far, 0), both_ways(y_far, 1)
    multiply_far(0, 256, late=False)
    c_arrived(6)
    multiply_far(0, 256, late=True)
    multiply_near(4, 0, 2)
    for segment in (0, 1):
        increment(segment)
        local(segment)
    for copy in started:
        copy.wait_send()
    both_ways(y_far, 2)
    multiply_far(256, 128)
    increment(2)
    both_ways(y_far, 3)
    multiply_last(0, 2, 0, 0, COLS)
    both_ways(y_far, 4)
    multiply_last(0, 2, 1, 1024, 256)
    increment(3)
    state[...] = memaug[4, :HD + 16].astype(BF16)
    multiply_last(0, 1, 1, 0, 1024)
    for j in (1, 2, 3):
        @pl.when(x + j < RING)
        def _():
            state_copy(j).start()
    multiply_last(1, 2, 1, 0, 1024)
    local(2)
    local(3)
    for j in (1, 2, 3):
        @pl.when(x >= j)
        def _():
            state_copy(j).wait_recv()
            before[:HD] += prior[j - 1, :HD].astype(F32)
            before[HD:] += prior[j - 1, HD:HD + 1].astype(F32)
    for segment in range(4):
        memory[segment] = (memaug[segment] + before[...]).astype(BF16)
    for copy in forwarded:
        copy.wait_send()
    for j in (1, 2, 3):
        @pl.when(x + j < RING)
        def _():
            state_copy(j).wait_send()


def share(gate, h):
    return jax.nn.sigmoid(jnp.full((1, HD), gate[h], F32))


def finish(sq, base, memory, gate, out, mixed, sem):
    copies = []
    for segment in range(TOK // SEG):
        rows = slice(segment * SEG, (segment + 1) * SEG)
        for h in range(GROUP):
            cols = slice(h * HD, (h + 1) * HD)
            both = lax.dot_general(
                sq[rows, cols], memory[segment], (((1,), (1,)), ((), ())), preferred_element_type=F32
            )
            part = share(gate, h)
            retrieved = both[:, :HD] / (both[:, HD:] + 1.0)
            mixed[rows, cols] = (part * retrieved + (1.0 - part) * base[rows, cols]).astype(BF16)
        copies.append(pltpu.make_async_copy(mixed.at[rows, :], out.at[0, rows, :], sem.at[segment]))
        copies[-1].start()
    for copy in copies:
        copy.wait()


def body(hidden_in, w_query, w_key, w_value, mem_gate):
    dma = pltpu.SemaphoreType.DMA
    anywhere = pl.BlockSpec(memory_space=pl.ANY)
    width = GROUP * HD
    results = pl.pallas_call(
        kernel,
        out_shape=(
            pltpu.VMEM((TOK, width), BF16),
            pltpu.VMEM((TOK, width), F32),
            pltpu.VMEM((4, 2 * HD, HD), BF16),
        ),
        in_specs=[anywhere] * 4,
        out_specs=[pl.BlockSpec(memory_space=pltpu.VMEM)] * 3,
        scratch_shapes=[
            pltpu.VMEM((16 * ROWS, COLS), BF16),
            pltpu.VMEM((RING, TOK, FEAT), BF16),
            pltpu.VMEM((TOK, COLS), F32),
            pltpu.VMEM((5, 2 * HD, HD), F32),
            pltpu.VMEM((HD + 16, HD), BF16),
            pltpu.VMEM((3, HD + 16, HD), BF16),
            pltpu.VMEM((2 * HD, HD), F32),
            dma((4,)), dma((2, 4)), dma((2, 4)), dma((2, 4, 3)), dma((2, 4, 3)),
            dma((7, 2)), dma((7, 2)), dma((7, 2)), dma((7, 2)),
            dma((8, 2)), dma((8, 2)), dma((2, 4)), dma((2, 4)), dma((2, 5)), dma((2, 5)),
            dma((3,)), dma((3,)),
        ],
        compiler_params=pltpu.CompilerParams(
            collective_id=0, has_side_effects=True, vmem_limit_bytes=LIMIT
        ),
    )(*[pltpu.with_memory_space_constraint(a, pltpu.HBM) for a in (hidden_in, w_query, w_key, w_value)])
    vmem = pl.BlockSpec(memory_space=pltpu.VMEM)
    return pl.pallas_call(
        finish,
        out_shape=jax.ShapeDtypeStruct((1, TOK, width), BF16),
        in_specs=[vmem, vmem, vmem, pl.BlockSpec(memory_space=pltpu.SMEM)],
        out_specs=anywhere,
        scratch_shapes=[pltpu.VMEM((TOK, width), BF16), dma((4,))],
        compiler_params=pltpu.CompilerParams(vmem_limit_bytes=8 << 20),
    )(*results, mem_gate)


def solution(mesh):
    return jax.shard_map(
        body,
        mesh=mesh,
        in_specs=(
            P("dp", "ctx", "head"),
            P("dp", "head"),
            P("dp", "head"),
            P("dp", "head"),
            P("head"),
        ),
        out_specs=P("dp", "ctx", "head"),
        check_vma=False,
    )
```

```python
import math

import jax
import jax.numpy as jnp
from jax import lax
from jax.experimental import pallas as pl
from jax.experimental.pallas import tpu as pltpu
from jax.sharding import PartitionSpec as P

HD = 128
SEG = 128
GROUP = 8
RINGZ = 8
RING = 4
ROWS = 512
COMMON = 192
QUARTER = 80
COLS = 1280
TOK = 512
FEAT = 2048
MESH = pl.DeviceIdType.MESH
LIMIT = 52 << 20
F32 = jnp.float32
BF16 = jnp.bfloat16


def kernel(
    hidden, w_query, w_key, w_value, sq, base, memory,
    w_all, h_all, acc, memaug, state, prior, before,
    load_sem, zq_s, zq_r, za_s, za_r, xq_s, xq_r, xf_s, xf_r,
    c_s, c_r, y_s, y_r, yf_s, yf_r, st_s, st_r,
):
    dp = lax.axis_index("dp")
    x = lax.axis_index("ctx")
    y = lax.axis_index("head")
    z, core = dp // 2, dp % 2

    def zdev(step):
        return {"dp": (z + RINGZ + step) % RINGZ * 2 + core}

    def xdev(step):
        return {"ctx": (x + RING + step) % RING}

    def ydev(step):
        return {"head": (y + RING + step) % RING}

    other = {"dp": z * 2 + 1 - core}
    SIGN = (1, -1)

    started, forwarded = [], []

    def send(src, dst, ssem, rsem, dev, held=None):
        copy = pltpu.make_async_remote_copy(
            src_ref=src, dst_ref=dst, send_sem=ssem, recv_sem=rsem,
            device_id=dev, device_id_type=MESH,
        )
        copy.start()
        (started if held is None else held).append(copy)

    def arrived(dst, ssem, rsem):
        pltpu.make_async_remote_copy(
            src_ref=dst, dst_ref=dst, send_sem=ssem, recv_sem=rsem,
            device_id=other, device_id_type=MESH,
        ).wait_recv()

    def block_of(step):
        return (z + RINGZ + step) % RINGZ * 2 + core

    def wrows(block, start, size):
        return w_all.at[pl.ds(pl.multiple_of(block * ROWS + start, 16), size), :]

    own = pl.multiple_of(dp * ROWS, ROWS)
    loads = [
        pltpu.make_async_copy(w_query, w_all.at[pl.ds(own, ROWS), 0:1024], load_sem.at[0]),
        pltpu.make_async_copy(w_key, w_all.at[pl.ds(own, ROWS), 1024:1152], load_sem.at[1]),
        pltpu.make_async_copy(w_value, w_all.at[pl.ds(own, ROWS), 1152:1280], load_sem.at[2]),
    ]
    loads.append(pltpu.make_async_copy(hidden.at[0], h_all.at[y], load_sem.at[3]))
    for load in loads:
        load.start()

    barrier = pltpu.get_barrier_semaphore()
    for peer in (zdev(1), zdev(-1), xdev(1), xdev(-1), xdev(2), ydev(1), ydev(-1), other):
        pl.semaphore_signal(barrier, inc=1, device_id=peer, device_id_type=MESH)
    pl.semaphore_wait(barrier, 8)

    def hrows(shard, start, size):
        return h_all.at[shard, pl.ds(start, size), :]

    def y_own(direction, segment):
        rows = segment * SEG, SEG
        send(
            hidden.at[0, pl.ds(*rows), :], hrows(y, *rows),
            y_s.at[direction, segment], y_r.at[direction, segment], ydev(SIGN[direction]),
        )

    def y_half(shard, direction, piece):
        if piece >= 3:
            columns = pl.ds((2 * direction + piece - 3) * ROWS, ROWS)
            return h_all.at[shard, pl.ds(3 * SEG, SEG), columns]
        return hrows(shard, piece * SEG + direction * SEG // 2, SEG // 2)

    def y_arrived(direction, segment):
        shard = (y + RING - SIGN[direction]) % RING
        arrived(
            hrows(shard, segment * SEG, SEG),
            y_s.at[direction, segment], y_r.at[direction, segment],
        )
        for piece in (3, 4) if segment == 3 else (segment,):
            half = y_half(shard, direction, piece)
            send(
                half, half, yf_s.at[direction, piece], yf_r.at[direction, piece],
                ydev(SIGN[direction]), forwarded,
            )

    def y_far(direction, piece):
        half = y_half((y + 2) % RING, direction, piece)
        arrived(half, yf_s.at[direction, piece], yf_r.at[direction, piece])

    for segment in range(4):
        y_own(0, segment), y_own(1, segment)

    def q_part(block, part, half):
        start, size = ((0, QUARTER), (0, 48), (48, 32), (0, 32), (32, 48))[half]
        return wrows(block, COMMON + part * QUARTER + start, size)

    def a_part(block, direction, step, piece):
        if step == 4:
            return wrows(block, direction * COMMON // 2, COMMON // 2)
        return wrows(block, (piece, 2 - piece)[direction] * COMMON // 3, COMMON // 3)

    def z_half(direction, step):
        return 0 if step < 4 else 1 + direction

    def zq_send(direction, step):
        block = block_of(-SIGN[direction] * (step - 1))
        part = q_part(block, x, z_half(direction, step))
        send(part, part, zq_s.at[direction, step - 1], zq_r.at[direction, step - 1], zdev(SIGN[direction]))

    def za_send(direction, step, piece):
        part = a_part(block_of(-SIGN[direction] * (step - 1)), direction, step, piece)
        sems = za_s.at[direction, step - 1, piece], za_r.at[direction, step - 1, piece]
        send(part, part, *sems, zdev(SIGN[direction]))

    def zq_arrived(direction, step):
        part = q_part(block_of(-SIGN[direction] * step), x, z_half(direction, step))
        arrived(part, zq_s.at[direction, step - 1], zq_r.at[direction, step - 1])
        if step < 4:
            zq_send(direction, step + 1)
        if step == 1:
            za_send(direction, 1, 2)

    def za_arrived(direction, step, piece):
        part = a_part(block_of(-SIGN[direction] * step), direction, step, piece)
        sems = za_s.at[direction, step - 1, piece], za_r.at[direction, step - 1, piece]
        arrived(part, *sems)
        if step < 3:
            za_send(direction, step + 1, piece)
        elif step == 3 and piece == 1:
            za_send(direction, 4, 0)

    def x_block(i):
        return block_of((-1, 1, -2, 2, -3, 3, 4)[i])

    def xq_send(i):
        part = q_part(x_block(i), x, 0)
        for direction in (0, 1):
            send(part, part, xq_s.at[i, direction], xq_r.at[i, direction], xdev(SIGN[direction]))

    def xq_arrived(i):
        for direction in (0, 1):
            source = (x + RING - SIGN[direction]) % RING
            whole = q_part(x_block(i), source, 0)
            arrived(whole, xq_s.at[i, direction], xq_r.at[i, direction])
            part = q_part(x_block(i), source, 1 + direction + i % 2 * 2)
            send(part, part, xf_s.at[i, direction], xf_r.at[i, direction], xdev(SIGN[direction]))

    def c_part(block, part):
        start, size = ((0, COMMON), (COMMON, ROWS - COMMON))[part]
        return wrows(block, start, size)

    def c_send(i, part):
        rows = c_part(dp if i == 7 else x_block(i), part)
        send(rows, rows, c_s.at[i, part], c_r.at[i, part], other)

    def xf_arrived(i):
        for direction in (0, 1):
            part = q_part(x_block(i), (x + 2) % RING, 1 + direction + i % 2 * 2)
            arrived(part, xf_s.at[i, direction], xf_r.at[i, direction])

    def c_arrived(i):
        block = dp if i == 7 else x_block(i)
        for part in (0, 1):
            arrived(c_part(block + 1 - 2 * core, part), c_s.at[i, part], c_r.at[i, part])

    far = (y + 2) % RING

    def multiply(row, rows, block, start=0, size=COLS):
        column = pl.multiple_of(block % 4 * ROWS, ROWS)
        acc[row:row + rows, start:start + size] += jnp.dot(
            h_all[block // 4, row:row + rows, pl.ds(column, ROWS)],
            w_all[pl.ds(pl.multiple_of(block * ROWS, ROWS), ROWS), start:start + size],
            preferred_element_type=F32,
        )

    def multiply_near(step, first, last):
        def one(i, carry):
            block = (z + RINGZ + (1 - i // 2 * 2) * step) % RINGZ * 2 + i % 2

            @pl.when(block // 4 != far)
            def _():
                multiply(0, TOK, block)

            return carry

        lax.fori_loop(first, last, one, 0)

    opposite = (z + 4) % RINGZ

    def multiply_far(row, rows, first=0, last=4, start=0, size=COLS, late=None):
        def one(i, carry):
            block = far * 4 + i
            if late is None:
                multiply(row, rows, block, start, size)
            else:
                @pl.when((block // 2 == opposite) == late)
                def _():
                    multiply(row, rows, block, start, size)
            return carry

        lax.fori_loop(first, last, one, 0)

    def feature(v):
        return jnp.where(v > 0, v + 1.0, jnp.exp(jnp.minimum(v, 0.0)))

    iota_q = lax.broadcasted_iota(jnp.int32, (SEG, SEG), 0)
    iota_k = lax.broadcasted_iota(jnp.int32, (SEG, SEG), 1)
    scale = 1.0 / math.sqrt(HD)

    def multiply_last(first, last, odd, start, size):
        def one(i, carry):
            multiply(384, 128, far * 4 + 2 * i + odd, start, size)
            return carry

        lax.fori_loop(first, last, one, 0)

    def keys_of(segment):
        rows = slice(segment * SEG, (segment + 1) * SEG)
        return acc[rows, 1024:1152].astype(BF16), acc[rows, 1152:1280].astype(BF16)

    def increment(segment):
        keys, values = keys_of(segment)
        wide = feature(keys.astype(F32))
        high = wide.astype(BF16)
        low = (wide - high.astype(F32)).astype(BF16)
        left = jnp.concatenate([values.astype(F32).T.astype(BF16), jnp.ones((HD, SEG), BF16)], axis=0)
        added = jnp.dot(left, high, preferred_element_type=F32) + jnp.dot(
            left, low, preferred_element_type=F32
        )
        memaug[segment + 1] = memaug[segment] + added

    def local(segment):
        rows = slice(segment * SEG, (segment + 1) * SEG)
        keys, values = keys_of(segment)
        values = jnp.concatenate([values, jnp.ones((SEG, HD), BF16)], axis=1)
        for h in range(GROUP):
            cols = slice(h * HD, (h + 1) * HD)
            query = acc[rows, cols].astype(BF16)
            scores = lax.dot_general(
                query, keys, (((1,), (1,)), ((), ())), preferred_element_type=F32
            ) * scale
            scores = jnp.where(iota_q >= iota_k, scores, -jnp.inf)
            top = jnp.max(scores, axis=1, keepdims=True)
            probs = jnp.exp(scores - top).astype(BF16)
            both = jnp.dot(probs, values, preferred_element_type=F32)
            base[rows, cols] = both[:, :HD] / both[:, HD:]
            sq[rows, cols] = feature(query.astype(F32)).astype(BF16)

    def state_copy(j):
        return pltpu.make_async_remote_copy(
            src_ref=state, dst_ref=prior.at[j - 1], send_sem=st_s.at[j - 1], recv_sem=st_r.at[j - 1],
            device_id=xdev(j), device_id_type=MESH,
        )

    def both_ways(f, *n):
        f(0, *n), f(1, *n)

    for load in loads:
        load.wait()
    both_ways(zq_send, 1)
    both_ways(za_send, 1, 0)
    both_ways(za_send, 1, 1)
    c_send(7, 0), c_send(7, 1)
    acc[...] = jnp.zeros_like(acc)
    memaug[0] = jnp.zeros((2 * HD, HD), F32)
    before[...] = jnp.zeros_like(before)

    both_ways(zq_arrived, 1)
    xq_send(0), xq_send(1)
    both_ways(za_arrived, 1, 0)
    xq_arrived(0)
    both_ways(y_arrived, 0)
    xq_arrived(1)
    both_ways(zq_arrived, 2)
    xq_send(2), xq_send(3)
    both_ways(za_arrived, 1, 1)
    xf_arrived(0)
    c_send(0, 1)
    both_ways(za_arrived, 1, 2)
    c_send(0, 0), c_send(1, 0)
    xf_arrived(1)
    c_send(1, 1)
    both_ways(y_arrived, 1)
    xq_arrived(2)
    both_ways(zq_arrived, 3)
    xq_arrived(3)
    xq_send(4), xq_send(5)
    both_ways(za_arrived, 2, 0)
    both_ways(za_arrived, 2, 1)
    xf_arrived(2), xf_arrived(3)
    c_send(2, 1), c_send(3, 1)
    both_ways(za_arrived, 2, 2)
    c_send(2, 0), c_send(3, 0)
    both_ways(y_arrived, 2)
    xq_arrived(4)
    both_ways(zq_arrived, 4)
    xq_send(6)
    xq_arrived(5)
    both_ways(za_arrived, 3, 0)
    both_ways(za_arrived, 3, 1)
    xf_arrived(4), xf_arrived(5)
    c_send(4, 1), c_send(5, 1)
    both_ways(y_arrived, 3)
    xq_arrived(6)
    for i in (7, 0, 1):
        c_arrived(i)
    multiply_near(0, 0, 2)
    both_ways(za_arrived, 3, 2)
    c_send(4, 0), c_send(5, 0)
    multiply_near(1, 0, 4)
    c_arrived(2), c_arrived(3)
    multiply_near(2, 0, 2)
    xf_arrived(6)
    c_send(6, 1)
    multiply_near(2, 2, 4)
    both_ways(za_arrived, 4, 0)
    c_send(6, 0)
    c_arrived(4), c_arrived(5)
    multiply_near(3, 0, 4)
    both_ways(y_far, 0), both_ways(y_far, 1)
    multiply_far(0, 256, late=False)
    c_arrived(6)
    multiply_far(0, 256, late=True)
    multiply_near(4, 0, 2)
    for segment in (0, 1):
        increment(segment)
        local(segment)
    for copy in started:
        copy.wait_send()
    both_ways(y_far, 2)
    multiply_far(256, 128)
    increment(2)
    both_ways(y_far, 3)
    multiply_last(0, 2, 0, 0, COLS)
    both_ways(y_far, 4)
    multiply_last(0, 2, 1, 1024, 256)
    increment(3)
    state[...] = memaug[4, :HD + 16].astype(BF16)
    multiply_last(0, 1, 1, 0, 1024)
    for j in (1, 2, 3):
        @pl.when(x + j < RING)
        def _():
            state_copy(j).start()
    multiply_last(1, 2, 1, 0, 1024)
    local(2)
    local(3)
    for j in (1, 2, 3):
        @pl.when(x >= j)
        def _():
            state_copy(j).wait_recv()
            before[:HD] += prior[j - 1, :HD].astype(F32)
            before[HD:] += prior[j - 1, HD:HD + 1].astype(F32)
    for segment in range(4):
        memory[segment] = (memaug[segment] + before[...]).astype(BF16)
    for copy in forwarded:
        copy.wait_send()
    for j in (1, 2, 3):
        @pl.when(x + j < RING)
        def _():
            state_copy(j).wait_send()


def share(gate, h):
    return jax.nn.sigmoid(jnp.full((1, HD), gate[h], F32))


def finish(sq, base, memory, gate, out, mixed, sem):
    copies = []
    for segment in range(TOK // SEG):
        rows = slice(segment * SEG, (segment + 1) * SEG)
        for h in range(GROUP):
            cols = slice(h * HD, (h + 1) * HD)
            both = lax.dot_general(
                sq[rows, cols], memory[segment], (((1,), (1,)), ((), ())), preferred_element_type=F32
            )
            part = share(gate, h)
            retrieved = both[:, :HD] / (both[:, HD:] + 1.0)
            mixed[rows, cols] = (part * retrieved + (1.0 - part) * base[rows, cols]).astype(BF16)
        copies.append(pltpu.make_async_copy(mixed.at[rows, :], out.at[0, rows, :], sem.at[segment]))
        copies[-1].start()
    for copy in copies:
        copy.wait()


def body(hidden_in, w_query, w_key, w_value, mem_gate):
    dma = pltpu.SemaphoreType.DMA
    anywhere = pl.BlockSpec(memory_space=pl.ANY)
    width = GROUP * HD
    results = pl.pallas_call(
        kernel,
        out_shape=(
            pltpu.VMEM((TOK, width), BF16),
            pltpu.VMEM((TOK, width), F32),
            pltpu.VMEM((4, 2 * HD, HD), BF16),
        ),
        in_specs=[anywhere] * 4,
        out_specs=[pl.BlockSpec(memory_space=pltpu.VMEM)] * 3,
        scratch_shapes=[
            pltpu.VMEM((16 * ROWS, COLS), BF16),
            pltpu.VMEM((RING, TOK, FEAT), BF16),
            pltpu.VMEM((TOK, COLS), F32),
            pltpu.VMEM((5, 2 * HD, HD), F32),
            pltpu.VMEM((HD + 16, HD), BF16),
            pltpu.VMEM((3, HD + 16, HD), BF16),
            pltpu.VMEM((2 * HD, HD), F32),
            dma((4,)), dma((2, 4)), dma((2, 4)), dma((2, 4, 3)), dma((2, 4, 3)),
            dma((7, 2)), dma((7, 2)), dma((7, 2)), dma((7, 2)),
            dma((8, 2)), dma((8, 2)), dma((2, 4)), dma((2, 4)), dma((2, 5)), dma((2, 5)),
            dma((3,)), dma((3,)),
        ],
        compiler_params=pltpu.CompilerParams(
            collective_id=0, has_side_effects=True, vmem_limit_bytes=LIMIT
        ),
    )(*[pltpu.with_memory_space_constraint(a, pltpu.HBM) for a in (hidden_in, w_query, w_key, w_value)])
    vmem = pl.BlockSpec(memory_space=pltpu.VMEM)
    return pl.pallas_call(
        finish,
        out_shape=jax.ShapeDtypeStruct((1, TOK, width), BF16),
        in_specs=[vmem, vmem, vmem, pl.BlockSpec(memory_space=pltpu.SMEM)],
        out_specs=anywhere,
        scratch_shapes=[pltpu.VMEM((TOK, width), BF16), dma((4,))],
        compiler_params=pltpu.CompilerParams(vmem_limit_bytes=8 << 20),
    )(*results, mem_gate)


def solution(mesh):
    return jax.shard_map(
        body,
        mesh=mesh,
        in_specs=(
            P("dp", "ctx", "head"),
            P("dp", "head"),
            P("dp", "head"),
            P("dp", "head"),
            P("head"),
        ),
        out_specs=P("dp", "ctx", "head"),
        check_vma=False,
    )
```
